256 devices in a mesh: pool: 8 (over z), tp: 32 (over x, y, core).
Axes of the slice: x: 4, y: 4, z: 8, core: 2. Of those that a mesh axis runs over, the one named last changes fastest.
Arguments:
- tokens: bfloat16 [4096, 8192], P(('pool', 'tp')), may hold values from -4 to 4
- lengths: int32 [8, 4], P('pool'), may hold values from 1 to 256, 512 in all within a row
- hit_pages: int32 [8, 4, 4], P('pool'), may hold values from 0 to 4095, as said below
- new_owner: int32 [8, 16], P('pool'), may hold values from 0 to 7, as said below
- w_query: bfloat16 [8192, 8192], P('pool', 'tp'), may hold values from -0.125 to 0.125
- w_keyval: bfloat16 [4096, 4096], P('pool', 'tp'), may hold values from -0.0625 to 0.0625
- w_out: bfloat16 [8192, 8192], P('tp', 'pool'), may hold values from -0.0625 to 0.0625
- pool_pages: bfloat16 [4096, 32, 2048], P('pool', 'tp'), may hold values from -65 to 65
Outputs:
- mixed: float32 [4096, 8192], P(('pool', 'tp'))
- new_store: bfloat16 [128, 32, 2048], P('pool', 'tp')
The draws below stay inside these ranges and needn't reach their ends.
Inputs may be any that keep to these rules, and one draw needn't show every extreme that they name: Page p of the pool lies on pool index p // 512. In every group g at most 6 of the 16 entries of hit_pages[g] lie on one pool index, and some pool index holds exactly 6 of them in every group. A page may appear more than once. `new_owner`: in every group at most 2 of its 16 pages go to one pool index, and some pool index receives exactly 2 from every group. Row g holds the lengths of the 4 requests packed in group g, in order, and sums to 512.
All inputs are finite; a program needn't handle non-finite values.
Results may differ from the reference program's by a relative error of at most 0.009.
Values may be sent and summed in bfloat16 or wider, within the bound.
No kernel may reach another device: no remote copies, remote signals or barrier semaphores. Data moves between devices by JAX's collectives and lax.ppermute only.
A program may use at most 64 MiB of HBM per device.

```python
import math
import jax
import jax.numpy as jnp
import numpy as np
from jax import lax

D = 8192
H = 64
KVH = 8
HD = 128
PAGE = 32
REQS = 4
HITS = 4
PAGES_DEV = 512
CAPF = 6
CAPN = 2
GROUP = 512
TOKENS = 4096
NEWP = 16
NHIT = 16
POOL_PAGES = 4096
KV_PART = 64
N_POOL = 8
N_TP = 32


def spread_owners(base_key, groups, count_items, owners, capacity):
    hot_owner = jax.random.randint(jax.random.fold_in(base_key, 1), (), 0, owners)
    seat_owner = jnp.arange((owners - 1) * capacity, dtype=jnp.int32) // capacity
    seat_owner = seat_owner + (seat_owner >= hot_owner).astype(jnp.int32)
    group_keys = jax.random.split(jax.random.fold_in(base_key, 2), groups)

    def one_group(group_key):
        chosen = jax.random.permutation(group_key, seat_owner)[:count_items - capacity]
        listed = jnp.concatenate([jnp.full((capacity,), hot_owner, jnp.int32), chosen])
        return jax.random.permutation(jax.random.fold_in(group_key, 3), listed)
    return jax.vmap(one_group)(group_keys)


def draw_hit_pages(key, part):
    base_key = jax.random.fold_in(key, 11)
    owners = spread_owners(base_key, N_POOL, REQS * HITS, N_POOL, CAPF)
    within = jax.random.randint(jax.random.fold_in(base_key, 5), (N_POOL, REQS * HITS), 0, PAGES_DEV)
    return (owners * PAGES_DEV + within).astype(jnp.int32).reshape(N_POOL, REQS, HITS)


def draw_new_owner(key, part):
    base_key = jax.random.fold_in(key, 23)
    return spread_owners(base_key, N_POOL, NEWP, N_POOL, CAPN).astype(jnp.int32)


def draw_pool_pages(key, part):
    base_key = jax.random.fold_in(key, 37)
    dims = (N_POOL * PAGES_DEV, PAGE, 2 * KVH * HD)
    first_key = jax.random.fold_in(base_key, 1)
    values = jnp.clip(jax.random.normal(first_key, dims, jnp.float32), -4.0, 4.0)
    values = values.reshape(dims[0], PAGE, N_TP, KV_PART).transpose(0, 2, 1, 3).reshape(dims[0], N_TP, PAGE * KV_PART)
    return values.astype(jnp.bfloat16)


def steps_of(stream_key, shape, cuts, least, high):
    loudness, own = 1.0, jax.random.fold_in(stream_key, 6)
    for dim, blocks in cuts:
        steps = jnp.exp(jax.random.uniform(jax.random.fold_in(own, dim), (blocks,), jnp.float32, least / len(cuts), high / len(cuts)))
        loudness = loudness * jnp.repeat(steps, shape[dim] // blocks).reshape([-1 if axis == dim else 1 for axis in range(len(shape))])
    return loudness


def length_profile(amount, total, most, slope):
    portions = [(1 << 20) // math.isqrt(standing ** slope) + 1 for standing in range(2, amount + 1)]
    rest, holding = total - most - (amount - 1), [1] * (amount - 1)
    while rest > 0:
        candidates = [i for i in range(amount - 1) if holding[i] < most]
        whole, budget = sum([portions[i] for i in candidates]), rest
        for i in candidates:
            extra = min(most - holding[i], max(1, budget * portions[i] // whole), rest)
            holding[i] = holding[i] + extra
            rest = rest - extra
    return np.array([most] + holding)


def uneven_parts(own_key, number_of, total, bound, lean):
    if number_of == 2:
        one = jax.random.randint(own_key, (), max(1, total - bound), min(bound, total - 1) + 1)
        return jnp.stack([one, total - one])
    tallies = jnp.asarray(length_profile(number_of, total, bound, lean), jnp.int32)
    couples = (number_of - 1) // 2
    source_of, receiver = tallies[1:1 + 2 * couples:2], tallies[2:2 + 2 * couples:2]
    slack = jnp.minimum(source_of - 1, bound - receiver)
    passed = jax.random.randint(jax.random.fold_in(own_key, 1), (couples,), 0, 1 << 20) % (slack + 1)
    tallies = tallies.at[1:1 + 2 * couples:2].set(source_of - passed).at[2:2 + 2 * couples:2].set(receiver + passed)
    return tallies[jax.random.permutation(jax.random.fold_in(own_key, 2), number_of)]


def bell_draw(key, extent, spread, reach, cuts=(), held_as=jnp.bfloat16):
    level = steps_of(key, extent, cuts, -0.22, 0.18) if cuts else 1.0
    result = jax.random.normal(key, extent, jnp.float32) * spread * level
    return jnp.minimum(jnp.maximum(result, -reach), reach).astype(held_as)


def setup_inputs(seed: int = 0) -> dict:
    splits = jax.random.split(jax.random.key(seed), 9)
    tokens = bell_draw(splits[0], (TOKENS, D), 0.5, 4.0, ((0, 256),))
    lengths = jax.vmap(lambda own: uneven_parts(own, REQS, GROUP, GROUP // 2, 2))(jax.random.split(splits[1], N_POOL)).reshape((N_POOL, REQS)).astype(jnp.int32)
    hit_pages = draw_hit_pages(jax.random.fold_in(splits[8], 71), 0)
    new_owner = draw_new_owner(jax.random.fold_in(splits[8], 71), 0)
    w_query = bell_draw(splits[4], (D, H * HD), (D // 4) ** -0.5, 0.125, ((0, 8), (1, 32)))
    w_keyval = bell_draw(splits[5], (D // 2, 2 * 2 * KVH * HD), D ** -0.5, 0.0625, ((0, 8), (1, 32)))
    w_out = bell_draw(splits[6], (H * HD, D), (H * HD) ** -0.5, 0.0625, ((0, 32), (1, 8)))
    pool_pages = draw_pool_pages(jax.random.fold_in(splits[8], 71), 0)
    return {"tokens": tokens, "lengths": lengths, "hit_pages": hit_pages, "new_owner": new_owner, "w_query": w_query, "w_keyval": w_keyval, "w_out": w_out, "pool_pages": pool_pages}


EPSILON = 1e-06
ROPE_BASE = 1000000.0

def rotate(values, positions):
    half = values.shape[-1] // 2
    steps_range = jnp.arange(half, dtype=jnp.float32)
    frequency = ROPE_BASE ** (-2.0 * steps_range / values.shape[-1])
    angles = positions.astype(jnp.float32)[:, None, None] * frequency[None, None, :]
    cosine = jnp.cos(angles)
    sine = jnp.sin(angles)
    first_half = values[..., :half]
    second_half = values[..., half:]
    return jnp.concatenate([first_half * cosine - second_half * sine, second_half * cosine + first_half * sine], axis=-1)

def request_layout(lengths_row):
    ends_at = jnp.cumsum(lengths_row).astype(jnp.int32)
    starts_at = (ends_at - lengths_row).astype(jnp.int32)
    token_index = jnp.arange(GROUP, dtype=jnp.int32)
    request_ids = lax.optimization_barrier(jnp.sum((token_index[:, None] >= ends_at[None, :]).astype(jnp.int32), axis=1)).astype(jnp.int32)
    chosen = request_ids[:, None] == jnp.arange(REQS, dtype=jnp.int32)[None, :]
    start_of = lax.optimization_barrier(jnp.sum(jnp.where(chosen, starts_at[None, :], 0), axis=1)).astype(jnp.int32)
    positions = token_index - start_of + HITS * PAGE
    return (token_index, request_ids, positions)

def slot_table(owners_row, capacity, seats):
    count_items = owners_row.shape[0]
    item_index = jnp.arange(count_items, dtype=jnp.int32)
    earlier_same = (owners_row[:, None] == owners_row[None, :]) & (item_index[None, :] < item_index[:, None])
    slots = lax.optimization_barrier(jnp.sum(earlier_same.astype(jnp.int32), axis=1)).astype(jnp.int32)
    targets = owners_row.astype(jnp.int32) * capacity + slots
    seat_index = jnp.arange(seats, dtype=jnp.int32)
    return targets[:, None] == seat_index[None, :]

def one_group(tokens_group, lengths_row, hits_row, owners_row, w_query, w_keyval, w_out, pool_pages):
    tokens_wide = tokens_group.astype(jnp.float32)
    normed = (tokens_wide * lax.rsqrt(lax.optimization_barrier(jnp.mean(tokens_wide * tokens_wide, axis=1, keepdims=True)) + EPSILON)).astype(jnp.bfloat16)
    token_index, request_ids, positions = request_layout(lengths_row)
    queries = jnp.dot(normed, w_query, preferred_element_type=jnp.float32).reshape(GROUP, H, HD)
    queries = rotate(queries, positions).astype(jnp.bfloat16)
    keyval = jnp.dot(normed, w_keyval, preferred_element_type=jnp.float32).astype(jnp.bfloat16).reshape(GROUP, KVH, 2 * HD)
    new_keys = rotate(keyval[:, :, :HD].astype(jnp.float32), positions).astype(jnp.bfloat16)
    new_kv = jnp.concatenate([new_keys, keyval[:, :, HD:]], axis=2)
    cached = jnp.take(pool_pages, hits_row.reshape(-1).astype(jnp.int32), axis=0).reshape(NHIT * PAGE, KVH, 2 * HD)
    all_kv = jnp.concatenate([cached, new_kv], axis=0).astype(jnp.float32)
    key_request = jnp.concatenate([jnp.arange(NHIT * PAGE, dtype=jnp.int32) // (HITS * PAGE), request_ids])
    key_order = jnp.concatenate([jnp.full((NHIT * PAGE,), -1, jnp.int32), token_index])
    visible = (request_ids[:, None] == key_request[None, :]) & (key_order[None, :] <= token_index[:, None])
    grouped = queries.astype(jnp.float32).reshape(GROUP, KVH, H // KVH, HD)
    scores = jnp.einsum('gjmd,kjd->jmgk', grouped, all_kv[:, :, :HD]) / math.sqrt(HD)
    scores = jnp.where(visible[None, None], scores, -jnp.inf)
    weights = lax.optimization_barrier(jax.nn.softmax(scores, axis=-1).astype(jnp.bfloat16)).astype(jnp.float32)
    attended = jnp.einsum('jmgk,kjd->gjmd', weights, all_kv[:, :, HD:]).reshape(GROUP, H * HD).astype(jnp.bfloat16)
    head_width = H * HD // N_TP
    head_pieces = attended.reshape(GROUP, N_TP, head_width).transpose(1, 0, 2)
    out_rows = w_out.reshape(N_TP, head_width, D)

    def add_part(running, weights_pair):
        term = jnp.dot(weights_pair[0], weights_pair[1], preferred_element_type=jnp.float32)
        term = lax.optimization_barrier(term.astype(jnp.bfloat16)).astype(jnp.float32)
        return (running + term, None)
    summed, _ignored = lax.scan(add_part, jnp.zeros((GROUP, D), jnp.float32), (head_pieces, out_rows))
    mixed = tokens_wide + summed
    new_pages = new_kv.reshape(NEWP, PAGE * KVH * 2 * HD)
    placed = slot_table(owners_row, CAPN, N_POOL * CAPN).astype(jnp.bfloat16)
    outgoing = jnp.dot(placed.T, new_pages, preferred_element_type=jnp.float32).astype(jnp.bfloat16)
    outgoing = outgoing.reshape(N_POOL, CAPN, PAGE, N_TP, KV_PART).transpose(0, 1, 3, 2, 4)
    return (mixed, outgoing.reshape(N_POOL, CAPN, N_TP, PAGE * KV_PART))

def reference(tokens, lengths, hit_pages, new_owner, w_query, w_keyval, w_out, pool_pages):
    keyval_matrix = w_keyval.reshape(D // 2, N_TP, 2, KV_PART).transpose(0, 2, 1, 3).reshape(D, 2 * KVH * HD)
    pages_plain = pool_pages.reshape(POOL_PAGES, N_TP, PAGE, KV_PART).transpose(0, 2, 1, 3).reshape(POOL_PAGES, PAGE, 2 * KVH * HD)

    def run_group(inputs):
        return one_group(inputs[0], inputs[1], inputs[2], inputs[3], w_query, keyval_matrix, w_out, pages_plain)
    mixed, outgoing = lax.map(run_group, (tokens.reshape(N_POOL, GROUP, D), lengths, hit_pages, new_owner))
    new_store = outgoing.transpose(1, 0, 2, 3, 4).reshape(N_POOL * N_POOL * CAPN, N_TP, PAGE * KV_PART)
    return (mixed.reshape(TOKENS, D), new_store)
```

```python
import math

import jax
import jax.numpy as jnp
from jax import lax
from jax.sharding import PartitionSpec as P

KVH = 8
HD = 128
PAGE = 32
REQS = 4
HITS = 4
CAPF = 6
CAPN = 2

EPSILON = 1e-06
ROPE_BASE = 1000000.0


F32 = jnp.float32
BF16 = jnp.bfloat16


def dot(a, b):
    return jnp.dot(a, b, preferred_element_type=F32)


def flip(value, mask_of):
    pairs = [(s, s ^ mask_of(s)) for s in range(lax.axis_size("tp"))]
    return lax.ppermute(value, "tp", pairs)


def swap_core(value):
    return flip(value, lambda s: 1)


def along_i(value, e):
    return flip(value, lambda s: e << 1 if s % 2 == 0 else e << 3)


def along_j(value, e):
    return flip(value, lambda s: e << 3 if s % 2 == 0 else e << 1)


def ring(value, step):
    n = lax.axis_size("pool")
    return lax.ppermute(value, "pool", [(s, (s + step) % n) for s in range(n)])


def gather_ring(own):
    half = own.shape[0] // 2
    up1, dn1 = ring(own, 1), ring(own, -1)
    up2, dn2 = ring(up1, 1), ring(dn1, -1)
    up3, dn3 = ring(up2, 1), ring(dn2, -1)
    up4, dn4 = ring(up3[:half], 1), ring(dn3[half:], -1)
    return {0: own, 7: up1, 1: dn1, 6: up2, 2: dn2, 5: up3, 3: dn3, 4: (up4, dn4)}


def rotate(values, positions):
    half = values.shape[-1] // 2
    steps_range = jnp.arange(half, dtype=F32)
    frequency = ROPE_BASE ** (-2.0 * steps_range / values.shape[-1])
    angles = positions.astype(F32)[:, None, None] * frequency[None, None, :]
    cosine = jnp.cos(angles)
    sine = jnp.sin(angles)
    first_half = values[..., :half]
    second_half = values[..., half:]
    return jnp.concatenate(
        [first_half * cosine - second_half * sine, second_half * cosine + first_half * sine],
        axis=-1,
    )


def slot_table(owners_row, item_index, capacity, seats):
    earlier_same = (owners_row[:, None] == owners_row[None, :]) & (
        item_index[None, :] < item_index[:, None]
    )
    slots = jnp.sum(earlier_same.astype(jnp.int32), axis=1)
    targets = owners_row * capacity + slots
    seat_index = jnp.arange(seats, dtype=jnp.int32)
    return targets[:, None] == seat_index[None, :]


def body(tokens, lengths, hit_pages, new_owner, w_query, w_keyval, w_out, pool_pages):
    rows_dev, width = tokens.shape
    tp_count = lax.axis_size("tp")
    pool_count = lax.axis_size("pool")
    tp_rank = lax.axis_index("tp")
    z = lax.axis_index("pool")
    core = tp_rank % 2
    chip = tp_rank // 2
    first_core = core == 0
    group_rows = rows_dev * tp_count
    chips = tp_count // 2
    query_width = w_query.shape[1]
    part_width = w_keyval.shape[1] // 2
    heads_here = query_width // HD
    sharing = tp_count // KVH
    pages_here = pool_pages.shape[0]
    slice_rows = w_query.shape[0]

    keyval_local = w_keyval.reshape(slice_rows, part_width)
    quarter = slice_rows // 4
    keyval_packed = jnp.concatenate(
        [keyval_local[n * quarter : (n + 1) * quarter] for n in range(4)], axis=1
    )
    shards = gather_ring(jnp.concatenate([w_query, keyval_packed], axis=0))

    tokens_wide = tokens.astype(F32)
    normed = (
        tokens_wide
        * lax.rsqrt(jnp.mean(tokens_wide * tokens_wide, axis=1, keepdims=True) + EPSILON)
    ).astype(BF16)
    rolled = lax.dynamic_slice_in_dim(
        jnp.concatenate([normed, normed], axis=1), z * slice_rows, width, 1
    )
    line = jnp.concatenate([rolled] + [along_j(rolled, e) for e in (1, 2, 3)], axis=0)
    own_rows = jnp.concatenate([line] + [along_i(line, e) for e in (1, 2, 3)], axis=0)
    other_rows = swap_core(own_rows)

    lengths_row = lengths[0]
    ends_at = jnp.cumsum(lengths_row)
    starts_at = ends_at - lengths_row
    row_index = jnp.arange(group_rows, dtype=jnp.int32)
    token_index = ((row_index // PAGE) ^ chip) * PAGE + row_index % PAGE
    request_ids = jnp.sum((token_index[:, None] >= ends_at[None, :]).astype(jnp.int32), axis=1)
    chosen = request_ids[:, None] == jnp.arange(REQS, dtype=jnp.int32)[None, :]
    start_of = jnp.sum(jnp.where(chosen, starts_at[None, :], 0), axis=1)
    positions = token_index - start_of + HITS * PAGE

    page_ids = hit_pages.reshape(-1)
    count_hits = page_ids.shape[0]
    hit_index = jnp.arange(count_hits, dtype=jnp.int32)
    placed_hits = slot_table(page_ids // pages_here, hit_index, CAPF, pool_count * CAPF)
    wanted = jnp.sum(jnp.where(placed_hits, (page_ids % pages_here)[:, None], 0), axis=0)
    wanted = wanted.reshape(pool_count, CAPF)
    asked = lax.all_to_all(wanted, "pool", split_axis=0, concat_axis=0, tiled=True)
    pages_flat = pool_pages.reshape(pages_here, pool_pages.shape[1] * pool_pages.shape[2])
    found = jnp.take(pages_flat, asked.reshape(-1), axis=0)
    found = found.reshape(asked.shape[0], asked.shape[1], pages_flat.shape[1])
    returned = lax.all_to_all(found, "pool", split_axis=0, concat_axis=0, tiled=True)
    returned = returned.reshape(pool_count * CAPF, PAGE * part_width)
    cached_part = dot(placed_hits.astype(BF16), returned).astype(BF16)
    cached_part = cached_part.reshape(count_hits * PAGE, part_width)

    keys_chip = tp_rank // 2 % 2 == 0

    def join_core(part):
        other = swap_core(part)
        return jnp.where(
            first_core,
            jnp.concatenate([part, other], axis=1),
            jnp.concatenate([other, part], axis=1),
        )

    def split_kv(mine, other):
        return jnp.where(keys_chip, mine, other), jnp.where(keys_chip, other, mine)

    cached_mine = join_core(cached_part)
    cached_keys, cached_values = split_kv(cached_mine, flip(cached_mine, lambda s: 2))

    def project(rows):
        total = None
        for d in (0, 7, 1, 6, 2, 5, 3, 4):
            shard = shards[d]
            if d == 4:
                shard = jnp.concatenate(shard, axis=0)
            keyval = jnp.concatenate(
                [shard[slice_rows:, n * part_width : (n + 1) * part_width] for n in range(4)], axis=0
            )
            weights = jnp.concatenate([shard[:slice_rows], keyval], axis=1)
            term = dot(rows[:, d * slice_rows : (d + 1) * slice_rows], weights)
            total = term if total is None else total + term
        return total

    own_out = project(own_rows).reshape(4, 4, rows_dev, query_width + part_width)
    other_out = project(other_rows).reshape(4, 4, rows_dev, query_width + part_width)
    core0 = jnp.where(first_core, own_out, other_out).transpose(1, 0, 2, 3)
    core1 = jnp.where(first_core, other_out, own_out)
    projected = jnp.stack([core0, core1], axis=2).reshape(group_rows, query_width + part_width)

    queries = rotate(
        projected[:, :query_width].reshape(group_rows, heads_here, HD), positions
    ).astype(BF16)
    keyval_part = projected[:, query_width:].astype(BF16)

    new_mine = join_core(keyval_part)
    new_other = flip(new_mine, lambda s: 2)
    new_other = new_other.reshape(chips // 2, 2, PAGE, HD)[:, ::-1].reshape(group_rows, HD)
    raw_keys, new_values = split_kv(new_mine, new_other)
    new_keys = (
        rotate(raw_keys.astype(F32).reshape(group_rows, 1, HD), positions)
        .astype(BF16)
        .reshape(group_rows, HD)
    )

    stored = jnp.where(keys_chip, new_keys, new_values)
    own_columns = jnp.where(first_core, stored[:, :part_width], stored[:, part_width:])
    page_rows = own_columns.reshape(chips, PAGE * part_width)
    page_index = jnp.arange(chips, dtype=jnp.int32) ^ chip
    placed_new = slot_table(
        jnp.take(new_owner[0], page_index), page_index, CAPN, pool_count * CAPN
    ).astype(BF16)
    outgoing = dot(placed_new.T, page_rows).astype(BF16)
    outgoing = outgoing.reshape(pool_count, CAPN, PAGE * part_width)
    new_store = lax.all_to_all(outgoing, "pool", split_axis=0, concat_axis=0, tiled=True).reshape(
        pool_count * CAPN, 1, PAGE * part_width
    )

    keys_all = jnp.concatenate([cached_keys, new_keys], axis=0)
    values_all = jnp.concatenate([cached_values, new_values], axis=0)
    cached_rows = count_hits * PAGE
    key_request = jnp.concatenate(
        [jnp.arange(cached_rows, dtype=jnp.int32) // (HITS * PAGE), request_ids]
    )
    key_order = jnp.concatenate([jnp.full((cached_rows,), -1, jnp.int32), token_index])
    scores = jnp.einsum("bhd,kd->hbk", queries, keys_all, preferred_element_type=F32) / math.sqrt(HD)
    visible = (request_ids[:, None] == key_request[None, :]) & (
        key_order[None, :] <= token_index[:, None]
    )
    scores = jnp.where(visible[None], scores, -jnp.inf)
    highest = jnp.max(scores, axis=-1, keepdims=True)
    expanded = jnp.exp(scores - highest)
    weights = (expanded / jnp.sum(expanded, axis=-1, keepdims=True)).astype(BF16)
    attended = (
        jnp.einsum("hbk,kd->bhd", weights, values_all, preferred_element_type=F32)
        .astype(BF16)
        .reshape(group_rows, query_width)
    )

    attended = jnp.concatenate([attended, swap_core(attended)], axis=1)
    by_chip = attended.reshape(4, 4, PAGE, 2 * query_width)
    attended = jnp.where(first_core, by_chip.transpose(1, 0, 2, 3), by_chip).reshape(
        group_rows, 2 * query_width
    )
    half_cols = w_out.shape[1] // 2
    left, right = w_out[:, :half_cols], w_out[:, half_cols:]
    kept = jnp.where(first_core, left, right)
    given = jnp.where(first_core, right, left)
    out_own = jnp.concatenate([kept, swap_core(given)], axis=0)
    out_own, _ = lax.optimization_barrier((out_own, shards[5]))
    out_shards = gather_ring(out_own)

    def reduce_chunk(ds):
        cols = [jnp.concatenate(out_shards[d], axis=0) if d == 4 else out_shards[d] for d in ds]
        part = dot(attended, jnp.concatenate(cols, axis=1)).astype(BF16)
        part = part.reshape(4, 4 * PAGE, len(ds) * half_cols)
        mine = part[0].astype(F32)
        for e in (1, 2, 3):
            mine = mine + along_i(part[e], e).astype(F32)
        mine = mine.astype(BF16).reshape(4, PAGE, len(ds) * half_cols)
        total = mine[0].astype(F32)
        for e in (1, 2, 3):
            total = total + along_j(mine[e], e).astype(F32)
        return total

    sums = {}
    for ds in ((7, 0, 1), (6, 2), (3, 4, 5)):
        total = reduce_chunk(ds).astype(BF16)
        keep = jnp.where(first_core, total[:rows_dev], total[rows_dev:])
        give = jnp.where(first_core, total[rows_dev:], total[:rows_dev])
        got = swap_core(give)
        for n, d in enumerate(ds):
            at = slice(n * half_cols, (n + 1) * half_cols)
            lo = jnp.where(first_core, keep[:, at], got[:, at])
            hi = jnp.where(first_core, got[:, at], keep[:, at])
            sums[d] = jnp.concatenate([lo, hi], axis=1)
    summed = jnp.concatenate([sums[d] for d in range(8)], axis=1)
    summed = lax.dynamic_slice_in_dim(
        jnp.concatenate([summed, summed], axis=1),
        (pool_count - z) % pool_count * slice_rows,
        width,
        1,
    )
    mixed = tokens_wide + summed.astype(F32)
    return (mixed, new_store)


def solution(mesh):
    return jax.shard_map(
        body,
        mesh=mesh,
        in_specs=(
            P(("pool", "tp"), None),
            P("pool", None),
            P("pool", None, None),
            P("pool", None),
            P("pool", "tp"),
            P("pool", "tp"),
            P("tp", "pool"),
            P("pool", "tp", None),
        ),
        out_specs=(P(("pool", "tp"), None), P("pool", "tp", None)),
        check_vma=False,
    )
```

```python
import math

import jax
import jax.numpy as jnp
from jax import lax
from jax.experimental import pallas as pl
from jax.experimental.pallas import tpu as pltpu
from jax.sharding import PartitionSpec as P


KVH = 8
HD = 128
PAGE = 32
REQS = 4
HITS = 4
CAPF = 6
CAPN = 2

EPSILON = 1e-06
ROPE_BASE = 1000000.0


F32 = jnp.float32
BF16 = jnp.bfloat16


def dot(a, b):
    return jnp.dot(a, b, preferred_element_type=F32)


def flip(value, mask_of):
    pairs = [(s, s ^ mask_of(s)) for s in range(lax.axis_size("tp"))]
    return lax.ppermute(value, "tp", pairs)


def swap_core(value):
    return flip(value, lambda s: 1)


def along_i(value, e):
    return flip(value, lambda s: e << 1 if s % 2 == 0 else e << 3)


def along_j(value, e):
    return flip(value, lambda s: e << 3 if s % 2 == 0 else e << 1)


def ring(value, step):
    n = lax.axis_size("pool")
    return lax.ppermute(value, "pool", [(s, (s + step) % n) for s in range(n)])


def gather_ring(own):
    half = own.shape[0] // 2
    up1, dn1 = ring(own, 1), ring(own, -1)
    up2, dn2 = ring(up1, 1), ring(dn1, -1)
    up3, dn3 = ring(up2, 1), ring(dn2, -1)
    up4, dn4 = ring(up3[:half], 1), ring(dn3[half:], -1)
    return {0: own, 7: up1, 1: dn1, 6: up2, 2: dn2, 5: up3, 3: dn3, 4: (up4, dn4)}


ANY = pl.BlockSpec(memory_space=pl.ANY)


def project_shards(pieces, shards, slices):
    count, depth, wide = len(shards), pieces[0].shape[1] // 8, shards[0].shape[1]
    rows = pieces[0].shape[0]
    total, part = rows * len(pieces), wide // 4
    first = slices[0]

    def kernel(*refs):
        piece_refs, refs = refs[: len(pieces)], refs[len(pieces) :]
        shard_refs, (query_ref, keyval_ref, held, buffer, sems) = refs[:count], refs[count:]
        k = pl.program_id(0)

        @pl.when(k == 0)
        def _():
            for n in range(count):
                pltpu.make_async_copy(shard_refs[n], buffer.at[n], sems.at[n]).start()
            query_ref[...] = jnp.zeros_like(query_ref)
            keyval_ref[...] = jnp.zeros_like(keyval_ref)

        for n, piece in enumerate(piece_refs):
            held[n * rows : (n + 1) * rows, :] = piece[...]
        pltpu.make_async_copy(shard_refs[0], buffer.at[k], sems.at[k]).wait()
        packed = buffer[k, depth:, :]
        keyval = jnp.concatenate([packed[:, n * part : (n + 1) * part] for n in range(4)], axis=0)
        query_ref[...] += dot(held[...], buffer[k, :depth, :])
        keyval_ref[...] += dot(held[...], keyval)

    return pl.pallas_call(
        kernel,
        grid=(count,),
        in_specs=[pl.BlockSpec((rows, depth), lambda k: (0, (k + first) % 8)) for _ in pieces]
        + [ANY] * count,
        out_specs=[
            pl.BlockSpec((total, wide), lambda k: (0, 0)),
            pl.BlockSpec((total, part), lambda k: (0, 0)),
        ],
        out_shape=[
            jax.ShapeDtypeStruct((total, wide), F32),
            jax.ShapeDtypeStruct((total, part), F32),
        ],
        scratch_shapes=[
            pltpu.VMEM((total, depth), BF16),
            pltpu.VMEM((count,) + shards[0].shape, BF16),
            pltpu.SemaphoreType.DMA((count,)),
        ],
        name="project_shards",
    )(*pieces, *shards)


def project_last(pieces, upper, lower, sums, cosine, sine, core):
    depth, wide = pieces[0].shape[1] // 8, upper.shape[1]
    rows = pieces[0].shape[0]
    total, part = rows * len(pieces), wide // 4
    cut = upper.shape[0]
    block_rows = total // 32

    def kernel(core_ref, *refs):
        piece_refs, refs = refs[: len(pieces)], refs[len(pieces) :]
        upper_ref, lower_ref, query_sum, keyval_sum, cos_ref, sin_ref = refs[:6]
        query_ref, keyval_ref, held, query_all, keyval_all = refs[6:]
        for n, piece in enumerate(piece_refs):
            held[n * rows : (n + 1) * rows, :] = piece[...]
        packed = lower_ref[depth - cut :, :]
        keyval = jnp.concatenate([packed[:, n * part : (n + 1) * part] for n in range(4)], axis=0)
        query_all[...] = (
            query_sum[...]
            + dot(held[:, :cut], upper_ref[...])
            + dot(held[:, cut:], lower_ref[: depth - cut, :])
        )
        keyval_all[...] = keyval_sum[...] + dot(held[...], keyval)
        own_core = core_ref[0]

        def place(b, carry):
            this_core = own_core ^ (b // 16)
            i, j = b // 4 % 4, b % 4
            across = jnp.where(this_core == 0, j, i)
            down = jnp.where(this_core == 0, i, j)
            source = pl.multiple_of(b * block_rows, block_rows)
            target = pl.multiple_of(((across * 4 + down) * 2 + this_core) * block_rows, block_rows)
            cos = cos_ref[pl.ds(target, block_rows), :]
            sin = sin_ref[pl.ds(target, block_rows), :]
            for h in range(wide // HD):
                v = query_all[pl.ds(source, block_rows), h * HD : (h + 1) * HD]
                turned = v * cos + pltpu.roll(v, HD // 2, 1) * sin
                query_ref[pl.ds(target, block_rows), h * HD : (h + 1) * HD] = turned.astype(BF16)
            keyval_ref[pl.ds(target, block_rows), :] = keyval_all[pl.ds(source, block_rows), :].astype(BF16)
            return carry

        lax.fori_loop(0, 32, place, 0)

    return pl.pallas_call(
        kernel,
        grid=(1,),
        in_specs=[pl.BlockSpec(memory_space=pltpu.SMEM)]
        + [pl.BlockSpec((rows, depth), lambda k: (0, 4)) for _ in pieces]
        + [pl.BlockSpec(a.shape, lambda k: (0, 0)) for a in (upper, lower, *sums, cosine, sine)],
        out_specs=[
            pl.BlockSpec((total, wide), lambda k: (0, 0)),
            pl.BlockSpec((total, part), lambda k: (0, 0)),
        ],
        out_shape=[
            jax.ShapeDtypeStruct((total, wide), BF16),
            jax.ShapeDtypeStruct((total, part), BF16),
        ],
        scratch_shapes=[
            pltpu.VMEM((total, depth), BF16),
            pltpu.VMEM((total, wide), F32),
            pltpu.VMEM((total, part), F32),
        ],
        name="project_last",
    )(core, *pieces, upper, lower, *sums, cosine, sine)


def output_blocks(attended, shards):
    count, (depth, wide) = len(shards), shards[0].shape
    rows = attended.shape[0] // 4

    def kernel(attended_ref, *refs):
        shard_refs, out_refs, (buffer, sems) = refs[:count], refs[count : count + 4], refs[count + 4 :]
        k = pl.program_id(0)

        @pl.when(k == 0)
        def _():
            for n in range(count):
                pltpu.make_async_copy(shard_refs[n], buffer.at[n], sems.at[n]).start()

        pltpu.make_async_copy(shard_refs[0], buffer.at[k], sems.at[k]).wait()
        product = dot(attended_ref[...], buffer[k]).astype(BF16)
        for n in range(4):
            out_refs[n][...] = product[n * rows : (n + 1) * rows]

    return pl.pallas_call(
        kernel,
        grid=(count,),
        in_specs=[pl.BlockSpec(attended.shape, lambda k: (0, 0))] + [ANY] * count,
        out_specs=[pl.BlockSpec((rows, wide), lambda k: (0, k))] * 4,
        out_shape=[jax.ShapeDtypeStruct((rows, count * wide), BF16)] * 4,
        scratch_shapes=[
            pltpu.VMEM((count, depth, wide), BF16),
            pltpu.SemaphoreType.DMA((count,)),
        ],
        name="output_blocks",
    )(attended, *shards)


def slot_table(owners_row, item_index, capacity, seats):
    earlier_same = (owners_row[:, None] == owners_row[None, :]) & (
        item_index[None, :] < item_index[:, None]
    )
    slots = jnp.sum(earlier_same.astype(jnp.int32), axis=1)
    targets = owners_row * capacity + slots
    seat_index = jnp.arange(seats, dtype=jnp.int32)
    return targets[:, None] == seat_index[None, :]


def block(tokens, lengths, hit_pages, new_owner, w_query, w_keyval, w_out, pool_pages):
    rows_dev, width = tokens.shape
    tp_count = lax.axis_size("tp")
    pool_count = lax.axis_size("pool")
    tp_rank = lax.axis_index("tp")
    z = lax.axis_index("pool")
    core = tp_rank % 2
    chip = tp_rank // 2
    first_core = core == 0
    group_rows = rows_dev * tp_count
    chips = tp_count // 2
    query_width = w_query.shape[1]
    part_width = w_keyval.shape[1] // 2
    heads_here = query_width // HD
    sharing = tp_count // KVH
    pages_here = pool_pages.shape[0]
    slice_rows = w_query.shape[0]

    quarter = slice_rows // 4
    keyval_local = w_keyval.reshape(slice_rows, part_width)
    keyval_packed = jnp.concatenate(
        [keyval_local[n * quarter : (n + 1) * quarter] for n in range(4)], axis=1
    )
    shards = gather_ring(jnp.concatenate([w_query, keyval_packed], axis=0))

    tokens_wide = tokens.astype(F32)
    normed = (
        tokens_wide
        * lax.rsqrt(jnp.mean(tokens_wide * tokens_wide, axis=1, keepdims=True) + EPSILON)
    ).astype(BF16)
    rolled = lax.dynamic_slice_in_dim(
        jnp.concatenate([normed, normed], axis=1), z * slice_rows, width, 1
    )
    line = jnp.concatenate([rolled] + [along_j(rolled, e) for e in (1, 2, 3)], axis=0)
    own_rows = [line] + [along_i(line, e) for e in (1, 2, 3)]
    other_rows = [swap_core(piece) for piece in own_rows]
    pieces = own_rows + other_rows

    lengths_row = lengths[0]
    ends_at = jnp.cumsum(lengths_row)
    starts_at = ends_at - lengths_row
    row_index = jnp.arange(group_rows, dtype=jnp.int32)
    token_index = ((row_index // PAGE) ^ chip) * PAGE + row_index % PAGE
    request_ids = jnp.sum((token_index[:, None] >= ends_at[None, :]).astype(jnp.int32), axis=1)
    chosen = request_ids[:, None] == jnp.arange(REQS, dtype=jnp.int32)[None, :]
    start_of = jnp.sum(jnp.where(chosen, starts_at[None, :], 0), axis=1)
    positions = token_index - start_of + HITS * PAGE

    page_ids = hit_pages.reshape(-1)
    count_hits = page_ids.shape[0]
    hit_index = jnp.arange(count_hits, dtype=jnp.int32)
    placed_hits = slot_table(page_ids // pages_here, hit_index, CAPF, pool_count * CAPF)
    wanted = jnp.sum(jnp.where(placed_hits, (page_ids % pages_here)[:, None], 0), axis=0)
    wanted = wanted.reshape(pool_count, CAPF)
    asked = lax.all_to_all(wanted, "pool", split_axis=0, concat_axis=0, tiled=True)
    pages_flat = pool_pages.reshape(pages_here, pool_pages.shape[1] * pool_pages.shape[2])
    found = jnp.take(pages_flat, asked.reshape(-1), axis=0)
    found = found.reshape(asked.shape[0], asked.shape[1], pages_flat.shape[1])
    returned = lax.all_to_all(found, "pool", split_axis=0, concat_axis=0, tiled=True)
    returned = returned.reshape(pool_count * CAPF, PAGE * part_width)
    cached_part = dot(placed_hits.astype(BF16), returned).astype(BF16)
    cached_part = cached_part.reshape(count_hits * PAGE, part_width)

    role = tp_rank % sharing

    def join(part, unflip):
        parts = [part] + [flip(part, lambda s, e=e: e) for e in (1, 2, 3)]
        parts[2:] = [unflip(p) for p in parts[2:]]

        def of(k):
            return jnp.where(
                role == k,
                parts[0],
                jnp.where(role == k ^ 1, parts[1], jnp.where(role == k ^ 2, parts[2], parts[3])),
            )

        return [of(k) for k in range(4)]

    cached = join(cached_part, lambda p: p)
    cached_keys = jnp.concatenate(cached[:2], axis=1)
    cached_values = jnp.concatenate(cached[2:], axis=1)

    steps_range = jnp.arange(HD // 2, dtype=F32)
    frequency = ROPE_BASE ** (-2.0 * steps_range / HD)
    angles = positions.astype(F32)[:, None] * frequency[None, :]
    cosine, sine = jnp.cos(angles), jnp.sin(angles)
    cosine = jnp.concatenate([cosine, cosine], axis=1)
    sine = jnp.concatenate([-sine, sine], axis=1)
    early = (5, 6, 7, 0, 1, 2, 3)
    sums = project_shards(pieces, [shards[d] for d in early], early)
    queries, keyval_part = project_last(
        pieces, *shards[4], sums, cosine, sine, core.astype(jnp.int32).reshape(1)
    )
    queries = queries.reshape(group_rows, heads_here, HD)

    def unflip(part):
        rows = part.reshape(chips // 2, 2, PAGE, part_width)
        return jnp.concatenate([rows[:, 1:], rows[:, :1]], axis=1).reshape(group_rows, part_width)

    new_parts = join(keyval_part, unflip)
    raw_keys = jnp.concatenate(new_parts[:2], axis=1)
    new_values = jnp.concatenate(new_parts[2:], axis=1)
    raw_keys = raw_keys.astype(F32)
    turned = jnp.concatenate([raw_keys[:, HD // 2 :], raw_keys[:, : HD // 2]], axis=1)
    new_keys = (raw_keys * cosine + turned * sine).astype(BF16)

    own_columns = jnp.where(
        role == 0,
        new_keys[:, :part_width],
        jnp.where(role == 1, new_keys[:, part_width:], keyval_part),
    )
    page_rows = own_columns.reshape(chips, PAGE * part_width)
    page_index = jnp.arange(chips, dtype=jnp.int32) ^ chip
    placed_new = slot_table(
        jnp.take(new_owner[0], page_index), page_index, CAPN, pool_count * CAPN
    ).astype(BF16)
    outgoing = dot(placed_new.T, page_rows).astype(BF16)
    outgoing = outgoing.reshape(pool_count, CAPN, PAGE * part_width)
    new_store = lax.all_to_all(outgoing, "pool", split_axis=0, concat_axis=0, tiled=True)
    new_store = new_store.reshape(pool_count * CAPN, 1, PAGE * part_width)

    keys_all = jnp.concatenate([cached_keys, new_keys], axis=0)
    values_all = jnp.concatenate([cached_values, new_values], axis=0)
    cached_rows = count_hits * PAGE
    key_request = jnp.concatenate(
        [jnp.arange(cached_rows, dtype=jnp.int32) // (HITS * PAGE), request_ids]
    )
    key_order = jnp.concatenate([jnp.full((cached_rows,), -1, jnp.int32), token_index])
    scores = jnp.einsum("bhd,kd->hbk", queries, keys_all, preferred_element_type=F32) / math.sqrt(HD)
    visible = (request_ids[:, None] == key_request[None, :]) & (
        key_order[None, :] <= token_index[:, None]
    )
    scores = jnp.where(visible[None], scores, -jnp.inf)
    highest = jnp.max(scores, axis=-1, keepdims=True)
    expanded = jnp.exp(scores - highest)
    weights = (expanded / jnp.sum(expanded, axis=-1, keepdims=True)).astype(BF16)
    attended = (
        jnp.einsum("hbk,kd->bhd", weights, values_all, preferred_element_type=F32)
        .astype(BF16)
        .reshape(group_rows, query_width)
    )

    attended = jnp.concatenate([attended, swap_core(attended)], axis=1)
    by_chip = attended.reshape(4, 4, PAGE, 2 * query_width)
    attended = jnp.where(first_core, by_chip.transpose(1, 0, 2, 3), by_chip).reshape(
        group_rows, 2 * query_width
    )
    half_cols = w_out.shape[1] // 2
    left, right = w_out[:, :half_cols], w_out[:, half_cols:]
    kept = jnp.where(first_core, left, right)
    given = jnp.where(first_core, right, left)
    out_own = jnp.concatenate([kept, swap_core(given)], axis=0)
    out_shards = gather_ring(out_own)

    def reduce_chunk(ds):
        cols = [jnp.concatenate(out_shards[d], axis=0) if d == 4 else out_shards[d] for d in ds]
        part = output_blocks(attended, cols)
        mine = part[0].astype(F32)
        for e in (1, 2, 3):
            mine = mine + along_i(part[e], e).astype(F32)
        mine = mine.astype(BF16).reshape(4, PAGE, len(ds) * half_cols)
        total = mine[0].astype(F32)
        for e in (1, 2, 3):
            total = total + along_j(mine[e], e).astype(F32)
        return total

    sums = {}
    for ds in ((6, 7, 0, 1, 2), (3, 4, 5)):
        total = reduce_chunk(ds).astype(BF16)
        keep = jnp.where(first_core, total[:rows_dev], total[rows_dev:])
        give = jnp.where(first_core, total[rows_dev:], total[:rows_dev])
        got = swap_core(give)
        for n, d in enumerate(ds):
            at = slice(n * half_cols, (n + 1) * half_cols)
            lo = jnp.where(first_core, keep[:, at], got[:, at])
            hi = jnp.where(first_core, got[:, at], keep[:, at])
            sums[d] = jnp.concatenate([lo, hi], axis=1)
    summed = jnp.concatenate([sums[d] for d in range(8)], axis=1)
    summed = lax.dynamic_slice_in_dim(
        jnp.concatenate([summed, summed], axis=1),
        (pool_count - z) % pool_count * slice_rows,
        width,
        1,
    )
    mixed = tokens_wide + summed.astype(F32)
    return (mixed, new_store)


def solution(mesh):
    return jax.shard_map(
        block,
        mesh=mesh,
        in_specs=(
            P(("pool", "tp"), None),
            P("pool", None),
            P("pool", None, None),
            P("pool", None),
            P("pool", "tp"),
            P("pool", "tp"),
            P("tp", "pool"),
            P("pool", "tp", None),
        ),
        out_specs=(P(("pool", "tp"), None), P("pool", "tp", None)),
        check_vma=False,
    )
```

```python
import math

import jax
import jax.numpy as jnp
from jax import lax
from jax.experimental import pallas as pl
from jax.experimental.pallas import tpu as pltpu
from jax.sharding import PartitionSpec as P


KVH = 8
HD = 128
PAGE = 32
REQS = 4
HITS = 4
CAPF = 6
CAPN = 2

EPSILON = 1e-06
ROPE_BASE = 1000000.0


F32 = jnp.float32
BF16 = jnp.bfloat16


def dot(a, b):
    return jnp.dot(a, b, preferred_element_type=F32)


ALONG_Y = [[(x * 4 + y) * 2 for y in range(4)] for x in range(4)]
ALONG_X = [[(x * 4 + y) * 2 for x in range(4)] for y in range(4)]
I_GROUPS = ALONG_Y + [[d + 1 for d in group] for group in ALONG_X]


def swap_core(value):
    return lax.ppermute(value, "tp", [(s, s ^ 1) for s in range(lax.axis_size("tp"))])


def along_i(value, e):
    pairs = [(s, s ^ (e << 1 if s % 2 == 0 else e << 3)) for s in range(lax.axis_size("tp"))]
    return lax.ppermute(value, "tp", pairs)


def along_j(value, e):
    pairs = [(s, s ^ (e << 3 if s % 2 == 0 else e << 1)) for s in range(lax.axis_size("tp"))]
    return lax.ppermute(value, "tp", pairs)


def exchange(blocks, groups):
    return lax.all_to_all(
        blocks, "tp", split_axis=0, concat_axis=0, axis_index_groups=groups, tiled=True
    )


ANY = pl.BlockSpec(memory_space=pl.ANY)


STEPS = 8
AHEAD = 2


def project(pieces, weights, cosine, sine, place):
    rows, width = pieces[0].shape
    total, wide = rows * len(pieces), weights.shape[1]
    depth, part, tall = width // STEPS, wide // 4, weights.shape[0] // STEPS
    block_rows = total // 32

    def kernel(place_ref, *refs):
        piece_refs, refs = refs[: len(pieces)], refs[len(pieces) :]
        w_ref, cos_ref, sin_ref, query_ref, keyval_ref, packed_ref = refs[:6]
        held, buffer, query_all, keyval_all, sems = refs[6:]

        def copies(step):
            weight_copy = pltpu.make_async_copy(
                w_ref.at[step * tall : (step + 1) * tall], buffer.at[step], sems.at[step, len(pieces)]
            )
            return [weight_copy] + [
                pltpu.make_async_copy(
                    piece.at[:, step * depth : (step + 1) * depth],
                    held.at[step, n * rows : (n + 1) * rows, :],
                    sems.at[step, n],
                )
                for n, piece in enumerate(piece_refs)
            ]

        for step in range(AHEAD):
            for copy in copies(step):
                copy.start()
        for step in range(STEPS):
            for copy in copies(step):
                copy.wait()
            if step + AHEAD < STEPS:
                for copy in copies(step + AHEAD):
                    copy.start()
            packed = buffer[step, depth:, :]
            keyval = jnp.concatenate([packed[:, n * part : (n + 1) * part] for n in range(4)], axis=0)
            term, small = dot(held[step], buffer[step, :depth, :]), dot(held[step], keyval)
            query_all[...] = term if step == 0 else query_all[...] + term
            keyval_all[...] = small if step == 0 else keyval_all[...] + small

        own_core, own_x, own_y = place_ref[0], place_ref[1], place_ref[2]

        def put(b, carry):
            this_core = own_core ^ (b // 16)
            e, j = b // 4 % 4, b % 4
            across = own_x ^ jnp.where(this_core == 0, j, e)
            down = own_y ^ jnp.where(this_core == 0, e, j)
            source = pl.multiple_of(b * block_rows, block_rows)
            target = pl.multiple_of(((across * 4 + down) * 2 + this_core) * block_rows, block_rows)
            cos = cos_ref[pl.ds(target, block_rows), :]
            sin = sin_ref[pl.ds(target, block_rows), :]
            for h in range(wide // HD):
                at = slice(h * HD, (h + 1) * HD)
                v = query_all[pl.ds(source, block_rows), at]
                turned = v * cos + pltpu.roll(v, HD // 2, 1) * sin
                query_ref[pl.ds(target, block_rows), at] = turned.astype(BF16)
            keyval_ref[pl.ds(target, block_rows), :] = keyval_all[pl.ds(source, block_rows), :].astype(
                BF16
            )
            return carry

        lax.fori_loop(0, 32, put, 0)
        packed_ref[...] = jnp.concatenate(
            [keyval_ref[: total // 2, :], keyval_ref[total // 2 :, :]], axis=1
        )

    return pl.pallas_call(
        kernel,
        in_specs=[pl.BlockSpec(memory_space=pltpu.SMEM)]
        + [ANY] * (len(pieces) + 1)
        + [pl.BlockSpec(memory_space=pltpu.VMEM)] * 2,
        out_shape=[
            jax.ShapeDtypeStruct((total, wide), BF16),
            jax.ShapeDtypeStruct((total, part), BF16),
            jax.ShapeDtypeStruct((total // 2, part * 2), BF16),
        ],
        scratch_shapes=[
            pltpu.VMEM((STEPS, total, depth), BF16),
            pltpu.VMEM((STEPS, tall, wide), BF16),
            pltpu.VMEM((total, wide), F32),
            pltpu.VMEM((total, part), F32),
            pltpu.SemaphoreType.DMA((STEPS, len(pieces) + 1)),
        ],
        name="project",
    )(place, *pieces, weights, cosine, sine)


ROW_BLOCK = 128


def attend(queries, cached_parts, new_parts, cosine, sine, token_request, key_request, place):
    rows, wide = queries.shape
    cached = cached_parts[0].shape[0] * 2
    part = HD // 2
    keys = cached + rows

    def kernel(place_ref, query_ref, *refs):
        cached_refs, new_refs, refs = refs[:4], refs[4:8], refs[8:]
        cos_ref, sin_ref, request_ref, key_request_ref, out_ref, new_key_ref, key_all, value_all = refs
        role = place_ref[3]

        def head(part_refs):
            near = [
                jnp.concatenate([ref[:, :part], ref[:, part:]], axis=0) for ref in part_refs
            ]

            def of(k):
                low = jnp.where(role == k, near[0], near[1])
                high = jnp.where(role == (k ^ 2), near[2], near[3])
                return jnp.where(role // 2 == k // 2, low, high)

            return (
                jnp.concatenate([of(0), of(1)], axis=1),
                jnp.concatenate([of(2), of(3)], axis=1),
            )

        key_all[:cached, :], value_all[:cached, :] = head(cached_refs)
        raw, new_values = head(new_refs)
        raw = raw.astype(F32)
        new_keys = (raw * cos_ref[...] + pltpu.roll(raw, HD // 2, 1) * sin_ref[...]).astype(BF16)
        key_all[cached:, :] = new_keys
        new_key_ref[...] = new_keys
        value_all[cached:, :] = new_values
        for first in range(0, rows, ROW_BLOCK):
            many = cached + first + ROW_BLOCK
            at = slice(first, first + ROW_BLOCK)
            token = first + lax.broadcasted_iota(jnp.int32, (ROW_BLOCK, many), 0)
            order = lax.broadcasted_iota(jnp.int32, (ROW_BLOCK, many), 1) - cached
            visible = (request_ref[at, :] == key_request_ref[:, :many]) & (order <= token)
            for h in range(wide // HD):
                columns = slice(h * HD, (h + 1) * HD)
                scores = lax.dot_general(
                    query_ref[at, columns],
                    key_all[:many, :],
                    (((1,), (1,)), ((), ())),
                    preferred_element_type=F32,
                ) * (1.0 / math.sqrt(HD))
                scores = jnp.where(visible, scores, -jnp.inf)
                expanded = jnp.exp(scores - jnp.max(scores, axis=1, keepdims=True))
                weights = expanded * (1.0 / jnp.sum(expanded, axis=1, keepdims=True))
                out_ref[at, columns] = dot(weights.astype(BF16), value_all[:many, :]).astype(BF16)

    vmem = pl.BlockSpec(memory_space=pltpu.VMEM)
    return pl.pallas_call(
        kernel,
        in_specs=[pl.BlockSpec(memory_space=pltpu.SMEM)] + [vmem] * 13,
        out_shape=[
            jax.ShapeDtypeStruct((rows, wide), BF16),
            jax.ShapeDtypeStruct((rows, HD), BF16),
        ],
        scratch_shapes=[pltpu.VMEM((keys, HD), BF16), pltpu.VMEM((keys, HD), BF16)],
        name="attend",
    )(place, queries, *cached_parts, *new_parts, cosine, sine, token_request, key_request)


def slot_table(owners_row, item_index, capacity, seats):
    earlier_same = (owners_row[:, None] == owners_row[None, :]) & (
        item_index[None, :] < item_index[:, None]
    )
    slots = jnp.sum(earlier_same.astype(jnp.int32), axis=1)
    targets = owners_row * capacity + slots
    seat_index = jnp.arange(seats, dtype=jnp.int32)
    return targets[:, None] == seat_index[None, :]


def block(tokens, lengths, hit_pages, new_owner, w_query, w_keyval, w_out, pool_pages):
    rows_dev, width = tokens.shape
    tp_count = lax.axis_size("tp")
    pool_count = lax.axis_size("pool")
    tp_rank = lax.axis_index("tp")
    core = tp_rank % 2
    first_core = core == 0
    place = jnp.stack([core, tp_rank // 8, tp_rank // 2 % 4, tp_rank % (tp_count // KVH)])
    group_rows = rows_dev * tp_count
    chips = tp_count // 2
    query_width = w_query.shape[1]
    part_width = w_keyval.shape[1] // 2
    sharing = tp_count // KVH
    pages_here = pool_pages.shape[0]
    slice_rows = w_query.shape[0]

    keyval_local = w_keyval.reshape(slice_rows, part_width)
    quarter = slice_rows // 4
    keyval_packed = jnp.concatenate(
        [keyval_local[n * quarter : (n + 1) * quarter] for n in range(4)], axis=1
    )
    gathered = lax.all_gather(
        jnp.concatenate([w_query, keyval_packed], axis=0), "pool", axis=0, tiled=True
    )

    tokens_wide = tokens.astype(F32)
    normed = (
        tokens_wide
        * lax.rsqrt(jnp.mean(tokens_wide * tokens_wide, axis=1, keepdims=True) + EPSILON)
    ).astype(BF16)
    line = jnp.concatenate([normed] + [along_j(normed, e) for e in (1, 2, 3)], axis=0)
    own_rows = [line] + [along_i(line, e) for e in (1, 2, 3)]
    other_rows = [swap_core(piece) for piece in own_rows]
    pieces = own_rows + other_rows

    lengths_row = lengths[0]
    ends_at = jnp.cumsum(lengths_row)
    starts_at = ends_at - lengths_row
    token_index = jnp.arange(group_rows, dtype=jnp.int32)
    request_ids = jnp.sum((token_index[:, None] >= ends_at[None, :]).astype(jnp.int32), axis=1)
    chosen = request_ids[:, None] == jnp.arange(REQS, dtype=jnp.int32)[None, :]
    start_of = jnp.sum(jnp.where(chosen, starts_at[None, :], 0), axis=1)
    positions = token_index - start_of + HITS * PAGE

    page_ids = hit_pages.reshape(-1)
    count_hits = page_ids.shape[0]
    hit_index = jnp.arange(count_hits, dtype=jnp.int32)
    placed_hits = slot_table(page_ids // pages_here, hit_index, CAPF, pool_count * CAPF)
    wanted = jnp.sum(jnp.where(placed_hits, (page_ids % pages_here)[:, None], 0), axis=0)
    wanted = wanted.reshape(pool_count, CAPF)
    asked = lax.all_to_all(wanted, "pool", split_axis=0, concat_axis=0, tiled=True)
    pages_flat = pool_pages.reshape(pages_here, pool_pages.shape[1] * pool_pages.shape[2])
    found = jnp.take(pages_flat, asked.reshape(-1), axis=0, mode="clip")
    found = found.reshape(asked.shape[0], asked.shape[1], pages_flat.shape[1])
    returned = lax.all_to_all(found, "pool", split_axis=0, concat_axis=0, tiled=True)
    returned = returned.reshape(pool_count * CAPF, PAGE * part_width)
    cached_part = dot(placed_hits.astype(BF16), returned).astype(BF16)
    cached_part = cached_part.reshape(count_hits * PAGE, part_width)
    cached_part = jnp.concatenate(
        [cached_part[: count_hits * PAGE // 2], cached_part[count_hits * PAGE // 2 :]], axis=1
    )

    role = tp_rank % sharing

    def around(part):
        return [part] + [
            lax.ppermute(part, "tp", [(s, s ^ e) for s in range(tp_count)]) for e in (1, 2, 3)
        ]

    cached_parts = around(cached_part)

    steps_range = jnp.arange(HD // 2, dtype=F32)
    frequency = ROPE_BASE ** (-2.0 * steps_range / HD)
    angles = positions.astype(F32)[:, None] * frequency[None, :]
    cosine, sine = jnp.cos(angles), jnp.sin(angles)
    cosine = jnp.concatenate([cosine, cosine], axis=1)
    sine = jnp.concatenate([-sine, sine], axis=1)
    queries, keyval_part, keyval_packed = project(pieces, gathered, cosine, sine, place)

    new_parts = around(keyval_packed)
    key_request = jnp.concatenate(
        [jnp.arange(count_hits * PAGE, dtype=jnp.int32) // (HITS * PAGE), request_ids]
    )
    attended, new_keys = attend(
        queries,
        cached_parts,
        new_parts,
        cosine,
        sine,
        request_ids[:, None],
        key_request[None, :],
        place,
    )

    own_columns = jnp.where(
        role == 0,
        new_keys[:, :part_width],
        jnp.where(role == 1, new_keys[:, part_width:], keyval_part),
    )
    page_rows = own_columns.reshape(chips, PAGE * part_width)
    page_index = jnp.arange(chips, dtype=jnp.int32)
    placed_new = slot_table(new_owner[0], page_index, CAPN, pool_count * CAPN).astype(BF16)
    outgoing = dot(placed_new.T, page_rows).astype(BF16)
    outgoing = outgoing.reshape(pool_count, CAPN, PAGE * part_width)
    new_store = lax.all_to_all(outgoing, "pool", split_axis=0, concat_axis=0, tiled=True)
    new_store = new_store.reshape(pool_count * CAPN, 1, PAGE * part_width)

    attended = jnp.concatenate([attended, swap_core(attended)], axis=1)
    attended = jnp.concatenate(
        [attended] + [along_i(attended, e) for e in (1, 2, 3)], axis=1
    )
    half_cols = w_out.shape[1] // 2
    quarter_cols = half_cols // 4
    left, right = w_out[:, :half_cols], w_out[:, half_cols:]
    kept = jnp.where(first_core, left, right)
    given = jnp.where(first_core, right, left)
    out_half = jnp.concatenate([kept, swap_core(given)], axis=0)
    quarters = jnp.concatenate(
        [out_half[:, n * quarter_cols : (n + 1) * quarter_cols] for n in range(4)], axis=0
    )
    out_own = exchange(quarters, I_GROUPS)
    own_i = jnp.where(first_core, tp_rank // 2 % 4, tp_rank // 8)
    depth = 2 * query_width
    out_own = jnp.concatenate(
        [lax.dynamic_slice_in_dim(out_own, (own_i ^ e) * depth, depth, 0) for e in range(4)], axis=0
    )
    full_out = lax.all_gather(out_own, "pool", axis=0, tiled=False)
    part = lax.dot_general(
        attended, full_out, (((1,), (1,)), ((), ())), preferred_element_type=F32
    ).astype(BF16)
    parts = lax.all_to_all(part, "tp", split_axis=0, concat_axis=0, tiled=True)
    parts = parts.reshape(4, 4, 2, rows_dev, pool_count, quarter_cols).astype(F32)
    low = jnp.sum(parts[:, :, 0], axis=0)
    high = jnp.sum(parts[:, :, 1], axis=1)
    summed = jnp.stack([low, high]).transpose(2, 3, 0, 1, 4).reshape(rows_dev, width)
    mixed = tokens_wide + summed.astype(F32)
    return (mixed, new_store)


def solution(mesh):
    return jax.shard_map(
        block,
        mesh=mesh,
        in_specs=(
            P(("pool", "tp"), None),
            P("pool", None),
            P("pool", None, None),
            P("pool", None),
            P("pool", "tp"),
            P("pool", "tp"),
            P("tp", "pool"),
            P("pool", "tp", None),
        ),
        out_specs=(P(("pool", "tp"), None), P("pool", "tp", None)),
        check_vma=False,
    )
```

```python
import math

import jax
import jax.numpy as jnp
from jax import lax
from jax.experimental import pallas as pl
from jax.experimental.pallas import tpu as pltpu
from jax.sharding import PartitionSpec as P


KVH = 8
HD = 128
PAGE = 32
REQS = 4
HITS = 4
CAPF = 6
CAPN = 2

EPSILON = 1e-06
ROPE_BASE = 1000000.0


F32 = jnp.float32
BF16 = jnp.bfloat16


def dot(a, b):
    return jnp.dot(a, b, preferred_element_type=F32)


ALONG_Y = [[(x * 4 + y) * 2 for y in range(4)] for x in range(4)]
ALONG_X = [[(x * 4 + y) * 2 for x in range(4)] for y in range(4)]
I_GROUPS = ALONG_Y + [[d + 1 for d in group] for group in ALONG_X]


def swap_core(value):
    return lax.ppermute(value, "tp", [(s, s ^ 1) for s in range(lax.axis_size("tp"))])


def along_i(value, e):
    pairs = [(s, s ^ (e << 1 if s % 2 == 0 else e << 3)) for s in range(lax.axis_size("tp"))]
    return lax.ppermute(value, "tp", pairs)


def along_j(value, e):
    pairs = [(s, s ^ (e << 3 if s % 2 == 0 else e << 1)) for s in range(lax.axis_size("tp"))]
    return lax.ppermute(value, "tp", pairs)


def exchange(blocks, groups):
    return lax.all_to_all(
        blocks, "tp", split_axis=0, concat_axis=0, axis_index_groups=groups, tiled=True
    )


ANY = pl.BlockSpec(memory_space=pl.ANY)


STEPS = 8
AHEAD = 2


def project(pieces, weights, cosine, sine, place):
    rows, width = pieces[0].shape
    total, wide = rows * len(pieces), weights.shape[1]
    depth, part, tall = width // STEPS, wide // 4, weights.shape[0] // STEPS
    block_rows = total // 32

    def kernel(place_ref, *refs):
        piece_refs, refs = refs[: len(pieces)], refs[len(pieces) :]
        w_ref, cos_ref, sin_ref, query_ref, keyval_ref, packed_ref = refs[:6]
        held, buffer, query_all, keyval_all, sems = refs[6:]

        def copies(step):
            weight_copy = pltpu.make_async_copy(
                w_ref.at[step * tall : (step + 1) * tall], buffer.at[step], sems.at[step, len(pieces)]
            )
            return [weight_copy] + [
                pltpu.make_async_copy(
                    piece.at[:, step * depth : (step + 1) * depth],
                    held.at[step, n * rows : (n + 1) * rows, :],
                    sems.at[step, n],
                )
                for n, piece in enumerate(piece_refs)
            ]

        for step in range(AHEAD):
            for copy in copies(step):
                copy.start()
        for step in range(STEPS):
            for copy in copies(step):
                copy.wait()
            if step + AHEAD < STEPS:
                for copy in copies(step + AHEAD):
                    copy.start()
            packed = buffer[step, depth:, :]
            keyval = jnp.concatenate([packed[:, n * part : (n + 1) * part] for n in range(4)], axis=0)
            term, small = dot(held[step], buffer[step, :depth, :]), dot(held[step], keyval)
            query_all[...] = term if step == 0 else query_all[...] + term
            keyval_all[...] = small if step == 0 else keyval_all[...] + small

        own_core, own_x, own_y = place_ref[0], place_ref[1], place_ref[2]

        def put(b, carry):
            this_core = own_core ^ (b // 16)
            e, j = b // 4 % 4, b % 4
            across = own_x ^ jnp.where(this_core == 0, j, e)
            down = own_y ^ jnp.where(this_core == 0, e, j)
            source = pl.multiple_of(b * block_rows, block_rows)
            target = pl.multiple_of(((across * 4 + down) * 2 + this_core) * block_rows, block_rows)
            cos = cos_ref[pl.ds(target, block_rows), :]
            sin = sin_ref[pl.ds(target, block_rows), :]
            for h in range(wide // HD):
                at = slice(h * HD, (h + 1) * HD)
                v = query_all[pl.ds(source, block_rows), at]
                turned = v * cos + pltpu.roll(v, HD // 2, 1) * sin
                query_ref[pl.ds(target, block_rows), at] = turned.astype(BF16)
            keyval_ref[pl.ds(target, block_rows), :] = keyval_all[pl.ds(source, block_rows), :].astype(
                BF16
            )
            return carry

        lax.fori_loop(0, 32, put, 0)
        packed_ref[...] = jnp.concatenate(
            [keyval_ref[: total // 2, :], keyval_ref[total // 2 :, :]], axis=1
        )

    return pl.pallas_call(
        kernel,
        in_specs=[pl.BlockSpec(memory_space=pltpu.SMEM)]
        + [ANY] * (len(pieces) + 1)
        + [pl.BlockSpec(memory_space=pltpu.VMEM)] * 2,
        out_shape=[
            jax.ShapeDtypeStruct((total, wide), BF16),
            jax.ShapeDtypeStruct((total, part), BF16),
            jax.ShapeDtypeStruct((total // 2, part * 2), BF16),
        ],
        scratch_shapes=[
            pltpu.VMEM((STEPS, total, depth), BF16),
            pltpu.VMEM((STEPS, tall, wide), BF16),
            pltpu.VMEM((total, wide), F32),
            pltpu.VMEM((total, part), F32),
            pltpu.SemaphoreType.DMA((STEPS, len(pieces) + 1)),
        ],
        name="project",
    )(place, *pieces, weights, cosine, sine)


ROW_BLOCK = 128


def attend(queries, cached_parts, new_parts, cosine, sine, token_request, key_request, place):
    rows, wide = queries.shape
    cached = cached_parts[0].shape[0] * 2
    part = HD // 2
    keys = cached + rows

    def kernel(place_ref, query_ref, *refs):
        cached_refs, new_refs, refs = refs[:4], refs[4:8], refs[8:]
        cos_ref, sin_ref, request_ref, key_request_ref, out_ref, new_key_ref, key_all, value_all = refs
        role = place_ref[3]

        def head(part_refs):
            near = [
                jnp.concatenate([ref[:, :part], ref[:, part:]], axis=0) for ref in part_refs
            ]

            def of(k):
                low = jnp.where(role == k, near[0], near[1])
                high = jnp.where(role == (k ^ 2), near[2], near[3])
                return jnp.where(role // 2 == k // 2, low, high)

            return (
                jnp.concatenate([of(0), of(1)], axis=1),
                jnp.concatenate([of(2), of(3)], axis=1),
            )

        key_all[:cached, :], value_all[:cached, :] = head(cached_refs)
        raw, new_values = head(new_refs)
        raw = raw.astype(F32)
        new_keys = (raw * cos_ref[...] + pltpu.roll(raw, HD // 2, 1) * sin_ref[...]).astype(BF16)
        key_all[cached:, :] = new_keys
        new_key_ref[...] = new_keys
        value_all[cached:, :] = new_values
        for first in range(0, rows, ROW_BLOCK):
            many = cached + first + ROW_BLOCK
            at = slice(first, first + ROW_BLOCK)
            token = first + lax.broadcasted_iota(jnp.int32, (ROW_BLOCK, many), 0)
            order = lax.broadcasted_iota(jnp.int32, (ROW_BLOCK, many), 1) - cached
            visible = (request_ref[at, :] == key_request_ref[:, :many]) & (order <= token)
            for h in range(wide // HD):
                columns = slice(h * HD, (h + 1) * HD)
                scores = lax.dot_general(
                    query_ref[at, columns],
                    key_all[:many, :],
                    (((1,), (1,)), ((), ())),
                    preferred_element_type=F32,
                ) * (1.0 / math.sqrt(HD))
                scores = jnp.where(visible, scores, -jnp.inf)
                expanded = jnp.exp(scores - jnp.max(scores, axis=1, keepdims=True))
                weights = expanded * (1.0 / jnp.sum(expanded, axis=1, keepdims=True))
                out_ref[at, columns] = dot(weights.astype(BF16), value_all[:many, :]).astype(BF16)

    vmem = pl.BlockSpec(memory_space=pltpu.VMEM)
    return pl.pallas_call(
        kernel,
        in_specs=[pl.BlockSpec(memory_space=pltpu.SMEM)] + [vmem] * 13,
        out_shape=[
            jax.ShapeDtypeStruct((rows, wide), BF16),
            jax.ShapeDtypeStruct((rows, HD), BF16),
        ],
        scratch_shapes=[pltpu.VMEM((keys, HD), BF16), pltpu.VMEM((keys, HD), BF16)],
        name="attend",
    )(place, queries, *cached_parts, *new_parts, cosine, sine, token_request, key_request)


def output_columns(attended, weights):
    count, tall, wide = weights.shape
    rows = attended.shape[0]
    pair = 2

    def kernel(attended_ref, weights_ref, out_ref):
        both = jnp.concatenate([weights_ref[m] for m in range(pair)], axis=1)
        out_ref[...] = dot(attended_ref[...], both).astype(BF16)

    return pl.pallas_call(
        kernel,
        grid=(count // pair,),
        in_specs=[
            pl.BlockSpec((rows, tall), lambda k: (0, 0)),
            pl.BlockSpec((pair, tall, wide), lambda k: (k, 0, 0)),
        ],
        out_specs=pl.BlockSpec((rows, pair * wide), lambda k: (0, k)),
        out_shape=jax.ShapeDtypeStruct((rows, count * wide), BF16),
        name="output_columns",
    )(attended, weights)


def slot_table(owners_row, item_index, capacity, seats):
    earlier_same = (owners_row[:, None] == owners_row[None, :]) & (
        item_index[None, :] < item_index[:, None]
    )
    slots = jnp.sum(earlier_same.astype(jnp.int32), axis=1)
    targets = owners_row * capacity + slots
    seat_index = jnp.arange(seats, dtype=jnp.int32)
    return targets[:, None] == seat_index[None, :]


def block(tokens, lengths, hit_pages, new_owner, w_query, w_keyval, w_out, pool_pages):
    rows_dev, width = tokens.shape
    tp_count = lax.axis_size("tp")
    pool_count = lax.axis_size("pool")
    tp_rank = lax.axis_index("tp")
    core = tp_rank % 2
    first_core = core == 0
    place = jnp.stack([core, tp_rank // 8, tp_rank // 2 % 4, tp_rank % (tp_count // KVH)])
    group_rows = rows_dev * tp_count
    chips = tp_count // 2
    query_width = w_query.shape[1]
    part_width = w_keyval.shape[1] // 2
    sharing = tp_count // KVH
    pages_here = pool_pages.shape[0]
    slice_rows = w_query.shape[0]

    keyval_local = w_keyval.reshape(slice_rows, part_width)
    quarter = slice_rows // 4
    keyval_packed = jnp.concatenate(
        [keyval_local[n * quarter : (n + 1) * quarter] for n in range(4)], axis=1
    )
    gathered = lax.all_gather(
        jnp.concatenate([w_query, keyval_packed], axis=0), "pool", axis=0, tiled=True
    )

    tokens_wide = tokens.astype(F32)
    normed = (
        tokens_wide
        * lax.rsqrt(jnp.mean(tokens_wide * tokens_wide, axis=1, keepdims=True) + EPSILON)
    ).astype(BF16)
    line = jnp.concatenate([normed] + [along_j(normed, e) for e in (1, 2, 3)], axis=0)
    own_rows = [line] + [along_i(line, e) for e in (1, 2, 3)]
    other_rows = [swap_core(piece) for piece in own_rows]
    pieces = own_rows + other_rows

    lengths_row = lengths[0]
    ends_at = jnp.cumsum(lengths_row)
    starts_at = ends_at - lengths_row
    token_index = jnp.arange(group_rows, dtype=jnp.int32)
    request_ids = jnp.sum((token_index[:, None] >= ends_at[None, :]).astype(jnp.int32), axis=1)
    chosen = request_ids[:, None] == jnp.arange(REQS, dtype=jnp.int32)[None, :]
    start_of = jnp.sum(jnp.where(chosen, starts_at[None, :], 0), axis=1)
    positions = token_index - start_of + HITS * PAGE

    page_ids = hit_pages.reshape(-1)
    count_hits = page_ids.shape[0]
    hit_index = jnp.arange(count_hits, dtype=jnp.int32)
    placed_hits = slot_table(page_ids // pages_here, hit_index, CAPF, pool_count * CAPF)
    wanted = jnp.sum(jnp.where(placed_hits, (page_ids % pages_here)[:, None], 0), axis=0)
    wanted = wanted.reshape(pool_count, CAPF)
    asked = lax.all_to_all(wanted, "pool", split_axis=0, concat_axis=0, tiled=True)
    pages_flat = pool_pages.reshape(pages_here, pool_pages.shape[1] * pool_pages.shape[2])
    found = jnp.take(pages_flat, asked.reshape(-1), axis=0, mode="clip")
    found = found.reshape(asked.shape[0], asked.shape[1], pages_flat.shape[1])
    returned = lax.all_to_all(found, "pool", split_axis=0, concat_axis=0, tiled=True)
    returned = returned.reshape(pool_count * CAPF, PAGE * part_width)
    cached_part = dot(placed_hits.astype(BF16), returned).astype(BF16)
    cached_part = cached_part.reshape(count_hits * PAGE, part_width)
    cached_part = jnp.concatenate(
        [cached_part[: count_hits * PAGE // 2], cached_part[count_hits * PAGE // 2 :]], axis=1
    )

    role = tp_rank % sharing

    def around(part):
        return [part] + [
            lax.ppermute(part, "tp", [(s, s ^ e) for s in range(tp_count)]) for e in (1, 2, 3)
        ]

    cached_parts = around(cached_part)

    steps_range = jnp.arange(HD // 2, dtype=F32)
    frequency = ROPE_BASE ** (-2.0 * steps_range / HD)
    angles = positions.astype(F32)[:, None] * frequency[None, :]
    cosine, sine = jnp.cos(angles), jnp.sin(angles)
    cosine = jnp.concatenate([cosine, cosine], axis=1)
    sine = jnp.concatenate([-sine, sine], axis=1)
    queries, keyval_part, keyval_packed = project(pieces, gathered, cosine, sine, place)

    new_parts = around(keyval_packed)
    key_request = jnp.concatenate(
        [jnp.arange(count_hits * PAGE, dtype=jnp.int32) // (HITS * PAGE), request_ids]
    )
    attended, new_keys = attend(
        queries,
        cached_parts,
        new_parts,
        cosine,
        sine,
        request_ids[:, None],
        key_request[None, :],
        place,
    )

    own_columns = jnp.where(
        role == 0,
        new_keys[:, :part_width],
        jnp.where(role == 1, new_keys[:, part_width:], keyval_part),
    )
    page_rows = own_columns.reshape(chips, PAGE * part_width)
    page_index = jnp.arange(chips, dtype=jnp.int32)
    placed_new = slot_table(new_owner[0], page_index, CAPN, pool_count * CAPN).astype(BF16)
    outgoing = dot(placed_new.T, page_rows).astype(BF16)
    outgoing = outgoing.reshape(pool_count, CAPN, PAGE * part_width)
    new_store = lax.all_to_all(outgoing, "pool", split_axis=0, concat_axis=0, tiled=True)
    new_store = new_store.reshape(pool_count * CAPN, 1, PAGE * part_width)

    attended = jnp.concatenate([attended, swap_core(attended)], axis=1)
    attended = jnp.concatenate(
        [attended] + [along_i(attended, e) for e in (1, 2, 3)], axis=1
    )
    half_cols = w_out.shape[1] // 2
    quarter_cols = half_cols // 4
    left, right = w_out[:, :half_cols], w_out[:, half_cols:]
    kept = jnp.where(first_core, left, right)
    given = jnp.where(first_core, right, left)
    out_half = jnp.concatenate([kept, swap_core(given)], axis=0)
    quarters = jnp.concatenate(
        [out_half[:, n * quarter_cols : (n + 1) * quarter_cols] for n in range(4)], axis=0
    )
    out_own = exchange(quarters, I_GROUPS)
    own_i = jnp.where(first_core, tp_rank // 2 % 4, tp_rank // 8)
    depth = 2 * query_width
    out_own = jnp.concatenate(
        [lax.dynamic_slice_in_dim(out_own, (own_i ^ e) * depth, depth, 0) for e in range(4)], axis=0
    )
    full_out = lax.all_gather(out_own, "pool", axis=0, tiled=False)
    part = output_columns(attended, full_out)
    parts = lax.all_to_all(part, "tp", split_axis=0, concat_axis=0, tiled=True)
    parts = parts.reshape(4, 4, 2, rows_dev, pool_count, quarter_cols).astype(F32)
    low = jnp.sum(parts[:, :, 0], axis=0)
    high = jnp.sum(parts[:, :, 1], axis=1)
    summed = jnp.stack([low, high]).transpose(2, 3, 0, 1, 4).reshape(rows_dev, width)
    mixed = tokens_wide + summed.astype(F32)
    return (mixed, new_store)


def solution(mesh):
    return jax.shard_map(
        block,
        mesh=mesh,
        in_specs=(
            P(("pool", "tp"), None),
            P("pool", None),
            P("pool", None, None),
            P("pool", None),
            P("pool", "tp"),
            P("pool", "tp"),
            P("tp", "pool"),
            P("pool", "tp", None),
        ),
        out_specs=(P(("pool", "tp"), None), P("pool", "tp", None)),
        check_vma=False,
    )
```
